32 devices in a mesh: dev: 32 (over z, y, x, core).
Axes of the slice: x: 2, y: 2, z: 4, core: 2. Of those that a mesh axis runs over, the one named last changes fastest.
Arguments:
- tokens: bfloat16 [32768, 384], P('dev'), may hold values from -6 to 6
- image_ids: int32 [32768], replicated, may hold values from 0 to 220, never falling along the last dimension, each value on 1 to 197 neighbouring positions
- cotangent: bfloat16 [32768, 384], P('dev'), may hold values from -6 to 6
- w_qkv: bfloat16 [2, 384, 1152], P(None, 'dev'), may hold values from -0.3125 to 0.3125
- bias_qv: bfloat16 [2, 768], P(None, 'dev'), may hold values from -3 to 3
- w_out: bfloat16 [2, 384, 384], P(None, 'dev'), may hold values from -1.25 to 1.25
- bias_out: bfloat16 [2, 384], P(None, 'dev'), may hold values from -3 to 3
- w_up: bfloat16 [2, 384, 1536], P(None, 'dev'), may hold values from -0.3125 to 0.3125
- bias_up: bfloat16 [2, 1536], P(None, 'dev'), may hold values from -3 to 3
- w_down: bfloat16 [2, 1536, 384], P(None, 'dev'), may hold values from -0.15625 to 0.15625
- bias_down: bfloat16 [2, 384], P(None, 'dev'), may hold values from -3 to 3
- norm1_gain: bfloat16 [2, 384], P(None, 'dev'), may hold values from 0.5 to 1.5
- norm1_shift: bfloat16 [2, 384], P(None, 'dev'), may hold values from -1.75 to 1.75
- norm2_gain: bfloat16 [2, 384], P(None, 'dev'), may hold values from 0.5 to 1.5
- norm2_shift: bfloat16 [2, 384], P(None, 'dev'), may hold values from -1.75 to 1.75
Outputs:
- output: bfloat16 [32768, 384], P('dev')
- grad_tokens: float32 [32768, 384], P('dev')
- grad_w_qkv: float32 [2, 384, 1152], P(None, 'dev')
- grad_bias_qv: float32 [2, 768], P(None, 'dev')
- grad_w_out: float32 [2, 384, 384], P(None, 'dev')
- grad_bias_out: float32 [2, 384], P(None, 'dev')
- grad_w_up: float32 [2, 384, 1536], P(None, 'dev')
- grad_bias_up: float32 [2, 1536], P(None, 'dev')
- grad_w_down: float32 [2, 1536, 384], P(None, 'dev')
- grad_bias_down: float32 [2, 384], P(None, 'dev')
- grad_norm1_gain: float32 [2, 384], P(None, 'dev')
- grad_norm1_shift: float32 [2, 384], P(None, 'dev')
- grad_norm2_gain: float32 [2, 384], P(None, 'dev')
- grad_norm2_shift: float32 [2, 384], P(None, 'dev')
The draws below stay inside these ranges and needn't reach their ends.
Inputs may be any that keep to these rules, and one draw needn't show every extreme that they name: `image_ids`: image ids never fall along the tokens, so each image is a run of consecutive tokens; every image holds 1 to 197 tokens and one holds exactly 197.
All inputs are finite; a program needn't handle non-finite values.
Results may differ from the reference program's by a relative error of at most 0.012.
Values may be sent and summed in bfloat16 or wider, within the bound.
No kernel may reach another device: no remote copies, remote signals or barrier semaphores. Data moves between devices by JAX's collectives and lax.ppermute only.
A program may use at most 192 MiB of HBM per device.

```python
import math
import jax
import jax.numpy as jnp
import numpy as np
from jax import lax

D = 384
HEADS = 6
HEAD_DIM = 64
FF = 1536
LAYERS = 2
IMG = 197
HALO = 256
QB = 512
TOKENS = 32768
IMAGES = 221


def block_levels(key, dims, cuts, smallest, high):
    level = 1.0
    for dim, parts in cuts:
        steps = jax.random.uniform(jax.random.fold_in(jax.random.fold_in(key, 6), dim), (parts,), jnp.float32, smallest / len(cuts), high / len(cuts))
        level = level * jnp.repeat(jnp.exp(steps), dims[dim] // parts).reshape((-1,) + (1,) * (len(dims) - 1 - dim))
    return level


def split_up(number_of, total, most, lean):
    portions = [(1 << 20) // math.isqrt(grade ** lean) + 1 for grade in range(2, number_of + 1)]
    rest, counts = total - most - (number_of - 1), [1] * (number_of - 1)
    while rest > 0:
        free = [i for i in range(number_of - 1) if counts[i] < most]
        whole, left = sum([portions[i] for i in free]), rest
        for i in free:
            addition = min(most - counts[i], max(1, left * portions[i] // whole), rest)
            counts[i] = counts[i] + addition
            rest = rest - addition
    return np.array([most] + counts)


def ragged_sizes(stream_key, number_of, total, limit, lean):
    if number_of == 2:
        one = jax.random.randint(stream_key, (), max(1, total - limit), min(limit, total - 1) + 1)
        return jnp.stack([one, total - one])
    tallies = jnp.asarray(split_up(number_of, total, limit, lean), jnp.int32)
    twos = (number_of - 1) // 2
    giver, receiver = tallies[1:1 + 2 * twos:2], tallies[2:2 + 2 * twos:2]
    margin = jnp.minimum(giver - 1, limit - receiver)
    moved = jax.random.randint(jax.random.fold_in(stream_key, 1), (twos,), 0, 1 << 20) % (margin + 1)
    tallies = tallies.at[1:1 + 2 * twos:2].set(giver - moved).at[2:2 + 2 * twos:2].set(receiver + moved)
    return tallies[jax.random.permutation(jax.random.fold_in(stream_key, 2), number_of)]


def noise(own_key, shape, scale, limit, shards=(), held_as=jnp.bfloat16):
    values = scale * jax.random.normal(own_key, shape, jnp.float32)
    if shards:
        values = values * block_levels(own_key, shape, shards, -0.22, 0.18)
    return jnp.clip(values, -limit, limit).astype(held_as)


def setup_inputs(seed: int = 0) -> dict:
    key_list = jax.random.split(jax.random.key(seed), 16)
    tokens = noise(key_list[0], (TOKENS, D), 1.0, 6.0, ((0, 32),))
    image_ids = jnp.searchsorted(jnp.cumsum(ragged_sizes(key_list[1], IMAGES, TOKENS, IMG, 1)), jnp.arange(TOKENS), side="right").astype(jnp.int32)
    cotangent = noise(key_list[2], (TOKENS, D), 1.0, 6.0, ((0, 32),))
    w_qkv = noise(key_list[3], (LAYERS, D, 3 * D), D ** -0.5, 0.3125, ((1, 32),))
    bias_qv = noise(key_list[4], (LAYERS, 2 * D), 0.5, 3.0, ((1, 32),))
    w_out = noise(key_list[5], (LAYERS, D, D), (D // 16) ** -0.5, 1.25, ((1, 32),))
    bias_out = noise(key_list[6], (LAYERS, D), 0.5, 3.0, ((1, 32),))
    w_up = noise(key_list[7], (LAYERS, D, FF), D ** -0.5, 0.3125, ((1, 32),))
    bias_up = noise(key_list[8], (LAYERS, FF), 0.5, 3.0, ((1, 32),))
    w_down = noise(key_list[9], (LAYERS, FF, D), FF ** -0.5, 0.15625, ((1, 32),))
    bias_down = noise(key_list[10], (LAYERS, D), 0.5, 3.0, ((1, 32),))
    norm1_gain = jnp.clip(1.0 + 0.1 * jax.random.normal(key_list[11], (LAYERS, D), jnp.float32), 0.5, 1.5).astype(jnp.bfloat16)
    norm1_shift = noise(key_list[12], (LAYERS, D), 0.3, 1.75, ((1, 32),))
    norm2_gain = jnp.clip(1.0 + 0.1 * jax.random.normal(key_list[13], (LAYERS, D), jnp.float32), 0.5, 1.5).astype(jnp.bfloat16)
    norm2_shift = noise(key_list[14], (LAYERS, D), 0.3, 1.75, ((1, 32),))
    return dict(tokens=tokens, image_ids=image_ids, cotangent=cotangent, w_qkv=w_qkv, bias_qv=bias_qv, w_out=w_out, bias_out=bias_out, w_up=w_up, bias_up=bias_up, w_down=w_down, bias_down=bias_down, norm1_gain=norm1_gain, norm1_shift=norm1_shift, norm2_gain=norm2_gain, norm2_shift=norm2_shift)


@jax.custom_vjp
def low(v):
    return lax.optimization_barrier(v.astype(jnp.bfloat16)).astype(jnp.float32)

@jax.custom_vjp
def low_back(v):
    return v

def low_keep(v):
    return (low(v), None)

def low_pass(kept, grad):
    return (grad,)

def back_keep(v):
    return (v, None)

def back_low(kept, grad):
    return (low(grad),)
low.defvjp(low_keep, low_pass)
low_back.defvjp(back_keep, back_low)

def layer_norm(values, gain, shift):
    centre = lax.optimization_barrier(jnp.mean(values, axis=-1, keepdims=True))
    centred = values - centre
    spread = lax.optimization_barrier(jnp.mean(centred * centred, axis=-1, keepdims=True))
    return centred * lax.rsqrt(spread + 1e-06) * gain + shift

def product(left, right):
    return jnp.dot(left, right, precision=lax.Precision.HIGHEST)

def attend_block(block_no, queries, padded, image_ids, padded_ids):
    first = block_no * QB
    window = QB + 2 * HALO
    query_block = lax.dynamic_slice_in_dim(queries, first, QB, 0).reshape(QB, HEADS, HEAD_DIM)
    key_window = lax.dynamic_slice_in_dim(padded, first, window, 0)
    key_heads = key_window[:, :D].reshape(window, HEADS, HEAD_DIM)
    value_heads = key_window[:, D:].reshape(window, HEADS, HEAD_DIM)
    id_query = lax.dynamic_slice_in_dim(image_ids, first, QB, 0)
    id_keys = lax.dynamic_slice_in_dim(padded_ids, first, window, 0)
    same_image = id_query[:, None] == id_keys[None, :]
    scores = jnp.einsum('qhd,khd->hqk', query_block, key_heads, precision=lax.Precision.HIGHEST) * 0.125
    scores = low_back(scores)
    scores = jnp.where(same_image[None], scores, -1e+30)
    soft = low(jax.nn.softmax(scores, axis=-1))
    attended = jnp.einsum('hqk,khd->qhd', soft, value_heads, precision=lax.Precision.HIGHEST)
    return attended.reshape(QB, D)

def attention(queries, keys, values, image_ids):
    keys_values = jnp.concatenate([keys, values], axis=1)
    rim_rows = jnp.zeros((HALO, 2 * D), jnp.float32)
    padded = jnp.concatenate([rim_rows, keys_values, rim_rows], axis=0)
    rim_ids = jnp.full((HALO,), -1, jnp.int32)
    padded_ids = jnp.concatenate([rim_ids, image_ids.astype(jnp.int32), rim_ids])
    block_fn = jax.checkpoint(attend_block)
    attended = lax.map(lambda block_no: block_fn(block_no, queries, padded, image_ids, padded_ids), jnp.arange(TOKENS // QB, dtype=jnp.int32))
    return attended.reshape(TOKENS, D)

def encoder_layer(stream, params, image_ids):
    w_qkv, bias_qv, w_out, bias_out, w_up, bias_up, w_down, bias_down, gain_one, shift_one, gain_two, shift_two = params
    normed = low(layer_norm(stream, gain_one, shift_one))
    mixed = product(normed, w_qkv)
    queries = low_back(low(mixed[:, :D] + bias_qv[:D]))
    keys = low_back(low(mixed[:, D:2 * D]))
    values = low_back(low(mixed[:, 2 * D:] + bias_qv[D:]))
    attended = low_back(low(attention(queries, keys, values, image_ids)))
    branch = low_back(product(attended, w_out) + bias_out)
    after = stream + branch
    normed_two = low(layer_norm(after, gain_two, shift_two))
    pre_hidden = low_back(product(normed_two, w_up) + bias_up)
    hidden = low(jax.nn.gelu(pre_hidden, approximate=False))
    branch_two = low_back(product(hidden, w_down) + bias_down)
    return after + branch_two

def reference(tokens, image_ids, cotangent, w_qkv, bias_qv, w_out, bias_out, w_up, bias_up, w_down, bias_down, norm1_gain, norm1_shift, norm2_gain, norm2_shift):
    params = tuple((item.astype(jnp.float32) for item in (w_qkv, bias_qv, w_out, bias_out, w_up, bias_up, w_down, bias_down, norm1_gain, norm1_shift, norm2_gain, norm2_shift)))
    start_stream = tokens.astype(jnp.float32)

    def forward(stream, *weights):
        for layer_no in range(LAYERS):
            stream = encoder_layer(stream, tuple((item[layer_no] for item in weights)), image_ids)
        return stream
    final, pullback = jax.vjp(forward, start_stream, *params)
    grads = pullback(cotangent.astype(jnp.float32))
    return (final.astype(jnp.bfloat16), grads[0], grads[1], grads[2], grads[3], grads[4], grads[5], grads[6], grads[7], grads[8], grads[9], grads[10], grads[11], grads[12])
```

```python
import functools

import jax
import jax.numpy as jnp
from jax import lax
from jax.experimental import pallas as pl
from jax.experimental.pallas import tpu as pltpu
from jax.sharding import PartitionSpec as P

D = 384
FF = 1536
LAYERS = 2
LONGEST = 197
HALO = 256
ROWS = 256
QB = 128
NARROW = 384
WIDE = 544
CHIPS = 16
EPSILON = 1e-06
NEGATIVE = -1e30
F32 = jnp.float32
BF16 = jnp.bfloat16

BIAS_QV, BIAS_OUT, BIAS_UP, BIAS_DOWN, GAIN_ONE, SHIFT_ONE, GAIN_TWO, SHIFT_TWO = range(8)
SIZES = (768, 384, 1536, 384, 384, 384, 384, 384)

VMEM_LIMIT = 60 * 1024 * 1024


def params():
    return pltpu.CompilerParams(
        dimension_semantics=("arbitrary",), vmem_limit_bytes=VMEM_LIMIT
    )


def mm(left, right):
    return jnp.dot(left, right, preferred_element_type=F32)


def mm_t(left, right):
    return lax.dot_general(left, right, (((1,), (1,)), ((), ())), preferred_element_type=F32)


def t_mm(left, right):
    return lax.dot_general(left, right, (((0,), (0,)), ((), ())), preferred_element_type=F32)


def normalize(values):
    centred = values - jnp.mean(values, axis=-1, keepdims=True)
    root = lax.rsqrt(jnp.mean(centred * centred, axis=-1, keepdims=True) + EPSILON)
    return centred * root, root


def normalize_back(grad, gain, unit, root):
    scaled = grad * gain
    return root * (
        scaled
        - jnp.mean(scaled, axis=-1, keepdims=True)
        - unit * jnp.mean(scaled * unit, axis=-1, keepdims=True)
    )


def column_sum(values):
    return jnp.sum(values.astype(F32), axis=0, keepdims=True)


def full(shape):
    return pl.BlockSpec(shape, lambda i, *_: (0,) * len(shape))


def once(shape):
    return pl.BlockSpec(shape, lambda i, *_: (0,) * len(shape), pipeline_mode=pl.Buffered(1))


def rows_of(width):
    return pl.BlockSpec((ROWS, width), lambda i, *_: (i, 0))


def shape(dims, dtype):
    return jax.ShapeDtypeStruct(dims, dtype)


def qkv_kernel(layer, pos, x_ref, own1, own2, oth1, oth2, vec, normed_ref, qkv_ref, w_ref):
    @pl.when(pl.program_id(0) == 0)
    def _():
        mine = pl.multiple_of(pos[32] * 768, 128)
        other = pl.multiple_of((1 - pos[32]) * 768, 128)
        for colour, base, pieces in (
            (0, mine, own1),
            (1, mine + 384, own2),
            (0, other, oth1),
            (1, other + 384, oth2),
        ):
            base = pl.multiple_of(base, 128)
            for j in range(CHIPS):
                row = pl.multiple_of(pos[16 * colour + j] * 24, 8)
                w_ref[pl.ds(row, 24), pl.ds(base, 384)] = pieces[24 * j : 24 * j + 24, :]

    base = 8 * layer
    unit, _root = normalize(x_ref[...].astype(F32))
    gain = vec[base + GAIN_ONE : base + GAIN_ONE + 1, :D]
    shift = vec[base + SHIFT_ONE : base + SHIFT_ONE + 1, :D]
    normed = (unit * gain + shift).astype(BF16)
    normed_ref[...] = normed
    bias = vec[base : base + 1, : 2 * D]
    qkv_ref[:, :D] = (mm(normed, w_ref[:, :D]) + bias[:, :D]).astype(BF16)
    qkv_ref[:, D : 2 * D] = mm(normed, w_ref[:, D : 2 * D]).astype(BF16)
    qkv_ref[:, 2 * D :] = (mm(normed, w_ref[:, 2 * D : 3 * D]) + bias[:, D:]).astype(BF16)


def qkv_call(layer, pos, x, pieces, vec):
    count = x.shape[0]
    return pl.pallas_call(
        functools.partial(qkv_kernel, layer),
        out_shape=(
            shape((count, D), BF16),
            shape((count, 3 * D), BF16),
            shape((D, 4 * D), BF16),
        ),
        grid_spec=pltpu.PrefetchScalarGridSpec(
            num_scalar_prefetch=1,
            grid=(count // ROWS,),
            in_specs=[rows_of(D)] + [once((D, D))] * 4 + [once((16, FF))],
            out_specs=[rows_of(D), rows_of(3 * D), full((D, 4 * D))],
        ),
        compiler_params=params(),
        cost_estimate=pl.CostEstimate(
            flops=2 * count * D * 3 * D, bytes_accessed=12 * count * D, transcendentals=0
        ),
        name="qkv",
    )(pos, x, *pieces, vec)


def paired(block):
    lane = lax.broadcasted_iota(jnp.int32, block.shape, 1)
    zero = jnp.zeros_like(block)
    return jnp.concatenate(
        [jnp.where(lane < 64, block, zero), jnp.where(lane < 64, zero, block)], axis=0
    )


def windows(spans, block, body):
    @pl.when(spans[2, block] == 1)
    def _():
        body(pl.multiple_of(spans[0, block], 16), NARROW)

    @pl.when(spans[2, block] == 0)
    def _():
        body(pl.multiple_of(spans[1, block], 16), WIDE)


def masks(id_col, id_row, first, width):
    same = id_col[pl.ds(first, width), :] == id_row[...]
    mask = jnp.where(same, 0.0, NEGATIVE)
    return jnp.concatenate([mask, mask], axis=1)


def attend_kernel(spans, qkv, id_col, id_row, out_ref, lse_ref):
    block = pl.program_id(0)
    row = pl.multiple_of(block * QB, QB)

    def body(first, width):
        mask = masks(id_col, id_row, first, width)
        for pair in range(3):
            lanes = slice(128 * pair, 128 * pair + 128)
            keys = qkv[pl.ds(first, width), D + 128 * pair : D + 128 * pair + 128]
            values = qkv[pl.ds(first, width), 2 * D + 128 * pair : 2 * D + 128 * pair + 128]
            queries = paired(qkv[pl.ds(row, QB), lanes] * jnp.asarray(0.125, BF16))
            scores = mm_t(keys, queries) + mask
            highest = jnp.max(scores, axis=0, keepdims=True)
            terms = jnp.exp(scores - highest)
            total = jnp.sum(terms, axis=0, keepdims=True)
            out = t_mm(values, terms.astype(BF16))
            inverse = 1.0 / total
            out_ref[128 * pair : 128 * pair + 64, :] = out[:64, :128] * inverse[:, :128]
            out_ref[128 * pair + 64 : 128 * pair + 128, :] = out[64:, 128:] * inverse[:, 128:]
            lse = highest + jnp.log(total)
            lse_ref[2 * pair : 2 * pair + 1, :] = lse[:, :128]
            lse_ref[2 * pair + 1 : 2 * pair + 2, :] = lse[:, 128:]

    windows(spans, block, body)


def attend_call(spans, qkv, id_col, id_row):
    count = qkv.shape[0]
    return pl.pallas_call(
        attend_kernel,
        out_shape=(shape((D, count), F32), shape((8, count), F32)),
        grid_spec=pltpu.PrefetchScalarGridSpec(
            num_scalar_prefetch=1,
            grid=(count // QB,),
            in_specs=[
                once((count, 3 * D)),
                once((count, 128)),
                pl.BlockSpec((1, QB), lambda i, *_: (0, i)),
            ],
            out_specs=[
                pl.BlockSpec((D, QB), lambda i, *_: (0, i)),
                pl.BlockSpec((8, QB), lambda i, *_: (0, i)),
            ],
        ),
        compiler_params=params(),
        cost_estimate=pl.CostEstimate(
            flops=4 * count * NARROW * D * 2, bytes_accessed=12 * count * D, transcendentals=0
        ),
        name="attend",
    )(spans, qkv, id_col, id_row)


def feed_kernel(
    layer, pos, x_ref, out_t, w_a, own1, own2, oth1, oth2, vec,
    after_ref, normed_ref, hidden_ref, slope_ref, result_ref, w_b, w_c,
):
    @pl.when(pl.program_id(0) == 0)
    def _():
        for half, up, down in ((pos[32], own1, own2), (1 - pos[32], oth1, oth2)):
            base = pl.multiple_of(half * 768, 128)
            for j in range(CHIPS):
                row = pl.multiple_of(pos[j] * 24, 8)
                w_b[pl.ds(row, 24), pl.ds(base, 384)] = up[48 * j : 48 * j + 24, :]
                w_b[pl.ds(row, 24), pl.ds(pl.multiple_of(base + 384, 128), 384)] = up[
                    48 * j + 24 : 48 * j + 48, :
                ]
                row = pl.multiple_of(pos[16 + j] * 96 + half * 48, 16)
                w_c[pl.ds(row, 48), :] = down[48 * j : 48 * j + 48, :]

    base = 8 * layer

    def small(which):
        return vec[base + which : base + which + 1, : SIZES[which]]

    attended = out_t[...].astype(BF16)
    after = x_ref[...].astype(F32) + t_mm(attended, w_a[:, 3 * D :]) + small(BIAS_OUT)
    after_ref[...] = after
    unit, _root = normalize(after)
    normed = (unit * small(GAIN_TWO) + small(SHIFT_TWO)).astype(BF16)
    normed_ref[...] = normed
    result = after + small(BIAS_DOWN)
    for start in range(0, FF, 512):
        lanes = slice(start, start + 512)
        pre = mm(normed, w_b[:, lanes]) + small(BIAS_UP)[:, lanes]
        chance = 0.5 + 0.5 * lax.erf(pre * 0.7071067811865476)
        density = 0.3989422804014327 * jnp.exp(-0.5 * pre * pre)
        hidden = (pre * chance).astype(BF16)
        hidden_ref[:, lanes] = hidden
        slope_ref[:, lanes] = (chance + pre * density).astype(BF16)
        result = result + mm(hidden, w_c[lanes, :])
    result_ref[...] = result.astype(result_ref.dtype)


def feed_call(layer, pos, x, out_t, w_a, pieces, vec, last):
    count = x.shape[0]
    return pl.pallas_call(
        functools.partial(feed_kernel, layer),
        out_shape=(
            shape((count, D), F32),
            shape((count, D), BF16),
            shape((count, FF), BF16),
            shape((count, FF), BF16),
            shape((count, D), BF16 if last else F32),
            shape((D, FF), BF16),
            shape((FF, D), BF16),
        ),
        grid_spec=pltpu.PrefetchScalarGridSpec(
            num_scalar_prefetch=1,
            grid=(count // ROWS,),
            in_specs=[
                rows_of(D),
                pl.BlockSpec((D, ROWS), lambda i, *_: (0, i)),
                once((D, 4 * D)),
            ]
            + [once((2 * D, D))] * 4
            + [once((16, FF))],
            out_specs=[
                rows_of(D), rows_of(D), rows_of(FF), rows_of(FF), rows_of(D),
                full((D, FF)), full((FF, D)),
            ],
        ),
        compiler_params=params(),
        cost_estimate=pl.CostEstimate(
            flops=2 * count * D * (D + 2 * FF), bytes_accessed=20 * count * D, transcendentals=0
        ),
        name="feed",
    )(pos, x, out_t, w_a, *pieces, vec)


def feed_back_kernel(
    layer, blocks, pos, grad_ref, hidden, slope_ref, normed, after_ref, out_t, w_a, w_b, w_c, vec,
    grad_after_ref, grad_att_ref, keep1, send1, keep2, send2, grad_out_ref, sums,
    pre_all, branch_all, out_all, up_sum, down_sum,
):
    step = pl.program_id(0)
    base = 8 * layer

    @pl.when(step == 0)
    def _():
        sums[...] = jnp.zeros_like(sums)

    def add(which, values):
        sums[which : which + 1, : SIZES[which]] += column_sum(values)

    rows = pl.ds(pl.multiple_of(step * ROWS, ROWS), ROWS)
    grad = grad_ref[...].astype(F32)
    branch = grad.astype(BF16)
    branch_all[rows, :] = branch
    add(BIAS_DOWN, branch)
    grad_normed = jnp.zeros((ROWS, D), F32)
    for start in range(0, FF, 512):
        lanes = slice(start, start + 512)
        pre = (mm_t(branch, w_c[lanes, :]) * slope_ref[:, lanes].astype(F32)).astype(BF16)
        pre_all[rows, lanes] = pre
        sums[BIAS_UP : BIAS_UP + 1, lanes] += column_sum(pre)
        grad_normed = grad_normed + mm_t(pre, w_b[:, lanes])
    unit, root = normalize(after_ref[...])
    add(GAIN_TWO, grad_normed * unit)
    add(SHIFT_TWO, grad_normed)
    gain = vec[base + GAIN_TWO : base + GAIN_TWO + 1, :D]
    grad_after = grad + normalize_back(grad_normed, gain, unit, root)
    grad_after_ref[...] = grad_after
    out_branch = grad_after.astype(BF16)
    out_all[rows, :] = out_branch
    add(BIAS_OUT, out_branch)
    grad_att_ref[...] = mm_t(out_branch, w_a[:, 3 * D :]).astype(BF16)

    @pl.when(step == blocks - 1)
    def _():
        for start in range(0, FF, 384):
            lanes = slice(start, start + 384)
            up_sum[:, lanes] = t_mm(normed[...], pre_all[:, lanes])
            down_sum[lanes, :] = t_mm(hidden[:, lanes], branch_all[...])
        grad_out_ref[...] = mm(out_t[...].astype(BF16), out_all[...])
        for half, up, down in ((pos[32], keep1, keep2), (1 - pos[32], send1, send2)):
            column = pl.multiple_of(half * 768, 128)
            for j in range(CHIPS):
                row = pl.multiple_of(pos[16 + j] * 24, 8)
                up[48 * j : 48 * j + 24, :] = up_sum[
                    pl.ds(row, 24), pl.ds(column, 384)
                ].astype(up.dtype)
                up[48 * j + 24 : 48 * j + 48, :] = up_sum[
                    pl.ds(row, 24), pl.ds(pl.multiple_of(column + 384, 128), 384)
                ].astype(up.dtype)
                row = pl.multiple_of(pos[j] * 96 + half * 48, 16)
                down[48 * j : 48 * j + 48, :] = down_sum[pl.ds(row, 48), :].astype(down.dtype)


def feed_back_call(layer, pos, grad, hidden, slope, normed, after, out_t, w_a, w_b, w_c, vec):
    count = grad.shape[0]
    blocks = count // ROWS
    return pl.pallas_call(
        functools.partial(feed_back_kernel, layer, blocks),
        out_shape=(
            shape((count, D), F32),
            shape((count, D), BF16),
            shape((2 * D, D), F32),
            shape((2 * D, D), BF16),
            shape((2 * D, D), F32),
            shape((2 * D, D), BF16),
            shape((D, D), F32),
            shape((8, FF), F32),
        ),
        grid_spec=pltpu.PrefetchScalarGridSpec(
            num_scalar_prefetch=1,
            grid=(blocks,),
            in_specs=[
                rows_of(D), once((count, FF)), rows_of(FF), once((count, D)), rows_of(D),
                once((D, count)), once((D, 4 * D)), once((D, FF)), once((FF, D)), once((16, FF)),
            ],
            out_specs=[rows_of(D), rows_of(D)]
            + [full((2 * D, D))] * 4
            + [full((D, D)), full((8, FF))],
            scratch_shapes=[
                pltpu.VMEM((count, FF), BF16),
                pltpu.VMEM((count, D), BF16),
                pltpu.VMEM((count, D), BF16),
                pltpu.VMEM((D, FF), F32),
                pltpu.VMEM((FF, D), F32),
            ],
        ),
        compiler_params=params(),
        cost_estimate=pl.CostEstimate(
            flops=4 * count * D * (D + 2 * FF), bytes_accessed=20 * count * D, transcendentals=0
        ),
        name="feed_back",
    )(pos, grad, hidden, slope, normed, after, out_t, w_a, w_b, w_c, vec)


def attend_back_kernel(
    blocks, spans, qkv, id_col, id_row, out_t, lse, grad_ref, grad_q, grad_kv, sums_kv
):
    block = pl.program_id(0)
    row = pl.multiple_of(block * QB, QB)

    @pl.when(block == 0)
    def _():
        sums_kv[...] = jnp.zeros_like(sums_kv)

    def body(first, width):
        mask = masks(id_col, id_row, first, width)
        for pair in range(3):
            lanes = slice(128 * pair, 128 * pair + 128)
            keys = qkv[pl.ds(first, width), D + 128 * pair : D + 128 * pair + 128]
            values = qkv[pl.ds(first, width), 2 * D + 128 * pair : 2 * D + 128 * pair + 128]
            queries = paired(qkv[pl.ds(row, QB), lanes] * jnp.asarray(0.125, BF16))
            grad = grad_ref[:, lanes]
            product = out_t[lanes, :] * jnp.transpose(grad.astype(F32))
            inner = jnp.concatenate([column_sum(product[:64]), column_sum(product[64:])], axis=1)
            grads = paired(grad)
            level = jnp.concatenate(
                [lse[2 * pair : 2 * pair + 1, :], lse[2 * pair + 1 : 2 * pair + 2, :]], axis=1
            )
            soft = jnp.exp(mm_t(keys, queries) + mask - level)
            grad_soft = mm_t(values, grads)
            grad_scores = (soft * (grad_soft - inner)).astype(BF16)
            window = pl.ds(first, width)
            sums_kv[window, lanes] += mm(grad_scores, queries)
            sums_kv[window, D + 128 * pair : D + 128 * pair + 128] += mm(soft.astype(BF16), grads)
            both = t_mm(keys, grad_scores)
            part = jnp.concatenate([both[:64, :128], both[64:, 128:]], axis=0)
            grad_q[:, lanes] = (jnp.transpose(part) * 0.125).astype(BF16)

    windows(spans, block, body)

    @pl.when(block == blocks - 1)
    def _():
        grad_kv[...] = sums_kv[...].astype(BF16)


def attend_back_call(spans, qkv, id_col, id_row, out_t, lse, grad):
    count = qkv.shape[0]
    blocks = count // QB
    return pl.pallas_call(
        functools.partial(attend_back_kernel, blocks),
        out_shape=(shape((count, D), BF16), shape((count, 2 * D), BF16)),
        grid_spec=pltpu.PrefetchScalarGridSpec(
            num_scalar_prefetch=1,
            grid=(blocks,),
            in_specs=[
                once((count, 3 * D)),
                once((count, 128)),
                pl.BlockSpec((1, QB), lambda i, *_: (0, i)),
                pl.BlockSpec((D, QB), lambda i, *_: (0, i)),
                pl.BlockSpec((8, QB), lambda i, *_: (0, i)),
                pl.BlockSpec((QB, D), lambda i, *_: (i, 0)),
            ],
            out_specs=[
                pl.BlockSpec((QB, D), lambda i, *_: (i, 0)),
                full((count, 2 * D)),
            ],
            scratch_shapes=[pltpu.VMEM((count, 2 * D), F32)],
        ),
        compiler_params=params(),
        cost_estimate=pl.CostEstimate(
            flops=10 * count * NARROW * D * 2, bytes_accessed=20 * count * D, transcendentals=0
        ),
        name="attend_back",
    )(spans, qkv, id_col, id_row, out_t, lse, grad)


def qkv_back_kernel(
    layer, blocks, pos, grad_q, grad_kv, normed, x_ref, grad_after, w_a, grad_out, vec,
    result_ref, keep1, send1, keep2, send2, sums, mixed_all, total,
):
    step = pl.program_id(0)
    base = 8 * layer

    @pl.when(step == 0)
    def _():
        sums[...] = jnp.zeros_like(sums)

    def add(which, values):
        sums[which : which + 1, : SIZES[which]] += column_sum(values)

    rows = pl.ds(pl.multiple_of(step * ROWS, ROWS), ROWS)
    mixed_all[rows, :D] = grad_q[...]
    mixed_all[rows, D:] = grad_kv[...]
    sums[BIAS_QV : BIAS_QV + 1, :D] += column_sum(grad_q[...])
    sums[BIAS_QV : BIAS_QV + 1, D : 2 * D] += column_sum(grad_kv[:, D:])
    grad_normed = mm_t(mixed_all[rows, :], w_a[:, : 3 * D])
    unit, root = normalize(x_ref[...].astype(F32))
    add(GAIN_ONE, grad_normed * unit)
    add(SHIFT_ONE, grad_normed)
    gain = vec[base + GAIN_ONE : base + GAIN_ONE + 1, :D]
    result_ref[...] = grad_after[...] + normalize_back(grad_normed, gain, unit, root)

    @pl.when(step == blocks - 1)
    def _():
        for start in range(0, 3 * D, 384):
            total[:, start : start + 384] = t_mm(normed[...], mixed_all[:, start : start + 384])
        total[:, 3 * D :] = grad_out[...]
        for half, one, two in ((pos[32], keep1, keep2), (1 - pos[32], send1, send2)):
            column = pl.multiple_of(half * 768, 128)
            for j in range(CHIPS):
                row = pl.multiple_of(pos[16 + j] * 24, 8)
                one[24 * j : 24 * j + 24, :] = total[
                    pl.ds(row, 24), pl.ds(column, 384)
                ].astype(one.dtype)
                row = pl.multiple_of(pos[j] * 24, 8)
                two[24 * j : 24 * j + 24, :] = total[
                    pl.ds(row, 24), pl.ds(pl.multiple_of(column + 384, 128), 384)
                ].astype(two.dtype)


def qkv_back_call(layer, pos, grad_q, grad_kv, normed, x, grad_after, w_a, grad_out, vec):
    count = x.shape[0]
    blocks = count // ROWS
    return pl.pallas_call(
        functools.partial(qkv_back_kernel, layer, blocks),
        out_shape=(
            shape((count, D), F32),
            shape((D, D), F32),
            shape((D, D), BF16),
            shape((D, D), F32),
            shape((D, D), BF16),
            shape((8, FF), F32),
        ),
        grid_spec=pltpu.PrefetchScalarGridSpec(
            num_scalar_prefetch=1,
            grid=(blocks,),
            in_specs=[
                rows_of(D), rows_of(2 * D), once((count, D)), rows_of(D), rows_of(D),
                once((D, 4 * D)), once((D, D)), once((16, FF)),
            ],
            out_specs=[rows_of(D)] + [full((D, D))] * 4 + [full((8, FF))],
            scratch_shapes=[pltpu.VMEM((count, 3 * D), BF16), pltpu.VMEM((D, 4 * D), F32)],
        ),
        compiler_params=params(),
        cost_estimate=pl.CostEstimate(
            flops=4 * count * D * 3 * D, bytes_accessed=20 * count * D, transcendentals=0
        ),
        name="qkv_back",
    )(pos, grad_q, grad_kv, normed, x, grad_after, w_a, grad_out, vec)


def place_kernel(widths, me, *refs):
    *parts, out_ref, table = refs
    table[...] = jnp.zeros_like(table)
    for layer in range(LAYERS):
        for which, (part, width) in enumerate(zip(parts, widths, strict=True)):
            table[8 * layer + which : 8 * layer + which + 1, :width] = part[
                layer : layer + 1, :
            ].astype(F32)
    row = lax.broadcasted_iota(jnp.int32, table.shape, 0) % 8
    result = jnp.zeros_like(table)
    for width in sorted(set(widths)):
        rolled = pltpu.roll(table[...], me[0] * width, 1)
        for which in range(8):
            if widths[which] == width:
                result = jnp.where(row == which, rolled, result)
    out_ref[...] = result.astype(out_ref.dtype)


def place_call(me, parts):
    widths = tuple(part.shape[1] for part in parts)
    return pl.pallas_call(
        functools.partial(place_kernel, widths),
        out_shape=shape((16, FF), F32),
        grid_spec=pltpu.PrefetchScalarGridSpec(
            num_scalar_prefetch=1,
            grid=(1,),
            in_specs=[full(part.shape) for part in parts],
            out_specs=full((16, FF)),
            scratch_shapes=[pltpu.VMEM((16, FF), F32)],
        ),
        compiler_params=params(),
        name="place",
    )(me, *parts)


def take_kernel(widths, me, table, *outs):
    for width in sorted(set(widths)):
        rolled = pltpu.roll(table[...], FF - me[0] * width, 1)
        for which, out in enumerate(outs):
            if widths[which] == width:
                for layer in range(LAYERS):
                    out[layer : layer + 1, :] = rolled[
                        8 * layer + which : 8 * layer + which + 1, :width
                    ]


def take_call(me, table, widths):
    return pl.pallas_call(
        functools.partial(take_kernel, widths),
        out_shape=tuple(shape((LAYERS, width), F32) for width in widths),
        grid_spec=pltpu.PrefetchScalarGridSpec(
            num_scalar_prefetch=1,
            grid=(1,),
            in_specs=[full((16, FF))],
            out_specs=[full((LAYERS, width)) for width in widths],
        ),
        compiler_params=params(),
        name="take",
    )(me, table)


def add_everywhere(table, count):
    bit = 1
    while bit < count:
        table = table + lax.ppermute(table, "dev", [(i, i ^ bit) for i in range(count)])
        bit *= 2
    return table


def swap(value, bit):
    count = lax.axis_size("dev")
    return lax.ppermute(value, "dev", [(i, i ^ bit) for i in range(count)])


def along_z(value, steps):
    moves = [(i, (i // 8 + steps) % 4 * 8 + i % 8) for i in range(32)]
    return lax.ppermute(value, "dev", moves)


CORE, X, Y = 1, 2, 4


def pack_kernel(pos, qkv, out, up, down, qkv2, out2, up2, *refs):
    *outs, table = refs
    core = pos[32]
    half = pl.multiple_of(core * 768, 128)

    def weave(column, mine, theirs, target, row):
        low = jnp.where(core == 0, mine, theirs)
        high = jnp.where(core == 0, theirs, mine)
        table[:12, :] = low.astype(F32)
        table[12:24, :] = high.astype(F32)
        target[row : row + 24, :] = table[:24, :].astype(BF16)

    for layer in range(LAYERS):
        a1, a2, f1, f2 = outs[4 * layer : 4 * layer + 4]

        def at(ref, column):
            return ref[layer, :, column : column + 384].astype(F32)

        first = core == 0
        weave(0, jnp.where(first, at(qkv, 0), at(qkv, 768)),
              jnp.where(first, at(qkv2, 0), at(qkv2, 768)), a1, 0)
        weave(0, jnp.where(first, at(qkv, 384), at(out, 0)),
              jnp.where(first, at(qkv2, 384), at(out2, 0)), a2, 0)
        for part in range(2):
            column = pl.ds(pl.multiple_of(half + 384 * part, 128), 384)
            weave(0, up[layer, :, column].astype(F32), up2[layer, :, column].astype(F32), f1, 24 * part)
        f2[...] = down[layer]


def pack_call(pos, mine, theirs):
    outs = [shape((24, D), BF16), shape((24, D), BF16), shape((48, D), BF16), shape((48, D), BF16)] * 2
    arrays = (*mine, *theirs)
    return pl.pallas_call(
        pack_kernel,
        out_shape=tuple(outs),
        grid_spec=pltpu.PrefetchScalarGridSpec(
            num_scalar_prefetch=1,
            grid=(1,),
            in_specs=[full(a.shape) for a in arrays],
            out_specs=[full(o.shape) for o in outs],
            scratch_shapes=[pltpu.VMEM((24, D), F32)],
        ),
        compiler_params=params(),
        name="pack",
    )(pos, *arrays)


def spread(piece, first, second):
    gathered = jnp.concatenate([piece] + [along_z(piece, -k) for k in range(1, 4)])
    gathered = jnp.concatenate([gathered, swap(gathered, first)])
    gathered = jnp.concatenate([gathered, swap(gathered, second)])
    return gathered, swap(gathered, CORE)


def collect(keep, send, first, second):
    total = keep + swap(send, CORE).astype(F32)
    for bit in (first, second):
        half = total.shape[0] // 2
        total = total[:half] + swap(total[half:].astype(BF16), bit).astype(F32)
    part = total.shape[0] // 4
    result = total[:part]
    for k in range(1, 4):
        result = result + along_z(total[part * k : part * k + part].astype(BF16), k).astype(F32)
    return result


def unpack_kernel(pos, *refs):
    ins, (qkv, out, up, down, table) = refs[: 7 * LAYERS], refs[7 * LAYERS :]
    core = pos[32]
    for layer in range(LAYERS):
        a1, a2, f1, f2, b1, b2, g1 = ins[7 * layer : 7 * layer + 7]

        def mine(ref, row):
            table[...] = ref[row : row + 24, :]
            return jnp.where(core == 0, table[:12, :], table[12:24, :])

        first = core == 0
        own_a1, own_a2, oth_a1, oth_a2 = mine(a1, 0), mine(a2, 0), mine(b1, 0), mine(b2, 0)
        qkv[layer, :, :384] = jnp.where(first, own_a1, oth_a1)
        qkv[layer, :, 384:768] = jnp.where(first, own_a2, oth_a2)
        qkv[layer, :, 768:] = jnp.where(first, oth_a1, own_a1)
        out[layer] = jnp.where(first, oth_a2, own_a2)
        for part in range(2):
            own, oth = mine(f1, 24 * part), mine(g1, 24 * part)
            up[layer, :, 384 * part : 384 * part + 384] = jnp.where(first, own, oth)
            up[layer, :, 768 + 384 * part : 768 + 384 * part + 384] = jnp.where(first, oth, own)
        down[layer] = f2[...]


def unpack_call(pos, arrays):
    outs = (
        shape((LAYERS, 12, 3 * D), F32), shape((LAYERS, 12, D), F32),
        shape((LAYERS, 12, FF), F32), shape((LAYERS, 48, D), F32),
    )
    return pl.pallas_call(
        unpack_kernel,
        out_shape=outs,
        grid_spec=pltpu.PrefetchScalarGridSpec(
            num_scalar_prefetch=1,
            grid=(1,),
            in_specs=[full(a.shape) for a in arrays],
            out_specs=[full(o.shape) for o in outs],
            scratch_shapes=[pltpu.VMEM((24, D), F32)],
        ),
        compiler_params=params(),
        name="unpack",
    )(pos, *arrays)


def gather_staged(pos, w_qkv, w_out, w_up, w_down):
    theirs = tuple(swap(w, CORE) for w in (w_qkv, w_out, w_up))
    packed = pack_call(pos, (w_qkv, w_out, w_up, w_down), theirs)
    layers = []
    for layer in range(LAYERS):
        a1, a2, f1, f2 = packed[4 * layer : 4 * layer + 4]
        (a1, b1), (a2, b2) = spread(a1, X, Y), spread(a2, Y, X)
        (f1, g1), (f2, g2) = spread(f1, X, Y), spread(f2, Y, X)
        layers.append(((a1, a2, b1, b2), (f1, f2, g1, g2)))
    return layers


def gather_plain(w_qkv, w_out, w_up, w_down):
    layers = []
    for layer in range(LAYERS):
        a, b, c = (
            lax.all_gather(w, "dev", axis=0, tiled=True)
            for w in (jnp.concatenate([w_qkv[layer], w_out[layer]], axis=1), w_up[layer], w_down[layer])
        )
        b = b.reshape(CHIPS, 24, 4, D).transpose(2, 0, 1, 3)
        ups = [jnp.stack([b[2 * h], b[2 * h + 1]], axis=1).reshape(2 * D, D) for h in range(2)]
        c = c.reshape(CHIPS, 2, 48, D)
        downs = [c[:, h].reshape(2 * D, D) for h in range(2)]
        layers.append(
            (tuple(a[:, D * k : D * k + D] for k in range(4)), (ups[0], downs[0], ups[1], downs[1]))
        )
    return layers


def reduce_plain(feeds, mixes):
    results = []
    for (k1, s1, k2, s2), (m1, t1, m2, t2) in zip(feeds, mixes, strict=True):
        a = jnp.concatenate([m1, m2, t1.astype(F32), t2.astype(F32)], axis=1)
        ups = [v.astype(F32).reshape(CHIPS, 2, 24, D) for v in (k1, s1)]
        b = jnp.concatenate([ups[h][:, p] for h in range(2) for p in range(2)], axis=-1)
        c = jnp.stack([v.astype(F32).reshape(CHIPS, 48, D) for v in (k2, s2)], axis=1)
        a, b, c = (
            lax.psum_scatter(v, "dev", scatter_dimension=0, tiled=True)
            for v in (a, b.reshape(D, FF), c.reshape(FF, D))
        )
        results.append((a[:, : 3 * D], a[:, 3 * D :], b, c))
    return tuple(jnp.stack([r[k] for r in results]) for k in range(4))


def on_device(
    tokens, image_ids, cotangent, w_qkv, bias_qv, w_out, bias_out, w_up, bias_up, w_down, bias_down,
    norm1_gain, norm1_shift, norm2_gain, norm2_shift,
):
    count = lax.axis_size("dev")
    staged = count == 32
    me = lax.axis_index("dev").astype(jnp.int32)
    own = tokens.shape[0]
    total = own + HALO
    small = (bias_qv, bias_out, bias_up, bias_down, norm1_gain, norm1_shift, norm2_gain, norm2_shift)
    widths = tuple(part.shape[1] for part in small)

    first_row = me * own
    everything = image_ids.shape[0]
    padding = everything + jnp.arange(HALO, dtype=jnp.int32)
    ids = lax.dynamic_slice_in_dim(jnp.concatenate([image_ids, padding]), first_row, total, 0)
    before = jnp.where(me == 0, -1, image_ids[jnp.maximum(first_row - 1, 0)])
    live = (ids > before) & (ids <= ids[own - 1])
    blocks = total // QB
    per_block = ids.reshape(blocks, QB)
    starts = jnp.sum((ids[None, :] < per_block[:, :1]).astype(jnp.int32), axis=1)
    ends = jnp.sum((ids[None, :] <= per_block[:, -1:]).astype(jnp.int32), axis=1)
    begin = starts // 16 * 16
    spans = jnp.stack(
        [
            jnp.minimum(begin, total - NARROW),
            jnp.minimum(begin, total - WIDE),
            (ends - begin <= NARROW).astype(jnp.int32),
        ]
    )
    id_row = ids[None, :]
    id_col = jnp.broadcast_to(ids[:, None], (total, 128))

    if staged:
        core, x, y, z = me % 2, me // 2 % 2, me // 4 % 2, me // 8
        j = jnp.arange(CHIPS, dtype=jnp.int32)
        depth, low, high = (z + j % 4) % 4 * 4, j // 4 % 2, j // 8
        pos = jnp.concatenate(
            [depth + (y ^ high) * 2 + (x ^ low), depth + (y ^ low) * 2 + (x ^ high), core[None]]
        )
        layers = gather_staged(pos, w_qkv, w_out, w_up, w_down)
    else:
        j = jnp.arange(CHIPS, dtype=jnp.int32)
        pos = jnp.concatenate([j, j, jnp.zeros((1,), jnp.int32)])
        layers = gather_plain(w_qkv, w_out, w_up, w_down)
    vec = add_everywhere(place_call(me[None], small), count)

    backward = [(i + 1, i) for i in range(count - 1)]
    forward = [(i, i + 1) for i in range(count - 1)]
    stream = jnp.concatenate([tokens, lax.ppermute(tokens[:HALO], "dev", backward)])
    grad = jnp.concatenate([cotangent, lax.ppermute(cotangent[:HALO], "dev", backward)])
    grad = jnp.where(live[:, None], grad, jnp.zeros_like(grad))

    saved = []
    for layer, (mix, feed) in enumerate(layers):
        normed_one, qkv, w_a = qkv_call(layer, pos, stream, mix, vec)
        out_t, lse = attend_call(spans, qkv, id_col, id_row)
        after, normed_two, hidden, slope, result, w_b, w_c = feed_call(
            layer, pos, stream, out_t, w_a, feed, vec, layer == LAYERS - 1
        )
        saved.append((stream, normed_one, qkv, w_a, out_t, lse, after, normed_two, hidden, slope, w_b, w_c))
        stream = result

    feeds, mixes, tables = [None] * LAYERS, [None] * LAYERS, [None] * LAYERS
    for layer in range(LAYERS - 1, -1, -1):
        x_in, normed_one, qkv, w_a, out_t, lse, after, normed_two, hidden, slope, w_b, w_c = saved[layer]
        grad_after, grad_att, k1, s1, k2, s2, grad_out, sums_one = feed_back_call(
            layer, pos, grad, hidden, slope, normed_two, after, out_t, w_a, w_b, w_c, vec
        )
        feeds[layer] = (k1, s1, k2, s2)
        if staged:
            feeds[layer] = (collect(k1, s1, X, Y), collect(k2, s2, Y, X))
        grad_q, grad_kv = attend_back_call(spans, qkv, id_col, id_row, out_t, lse, grad_att)
        grad, m1, t1, m2, t2, sums_two = qkv_back_call(
            layer, pos, grad_q, grad_kv, normed_one, x_in, grad_after, w_a, grad_out, vec
        )
        mixes[layer] = (m1, t1, m2, t2)
        if staged:
            mixes[layer] = (collect(m1, t1, X, Y), collect(m2, t2, Y, X))
        tables[layer] = sums_one + sums_two

    smalls = take_call(me[None], add_everywhere(jnp.concatenate(tables), count), widths)
    if staged:
        arrays = []
        for (f1, f2), (a1, a2) in zip(feeds, mixes, strict=True):
            arrays += [a1, a2, f1, f2, swap(a1, CORE), swap(a2, CORE), swap(f1, CORE)]
        large = unpack_call(pos, arrays)
    else:
        large = reduce_plain(feeds, mixes)

    def returned(values, dtype):
        came = lax.ppermute(values[own:].astype(BF16), "dev", forward).astype(dtype)
        head = jnp.where(live[:HALO, None], values[:HALO], came)
        return jnp.concatenate([head, values[HALO:own]])

    return (
        returned(stream, BF16), returned(grad, F32), large[0], smalls[0], large[1], smalls[1],
        large[2], smalls[2], large[3], smalls[3], smalls[4], smalls[5], smalls[6], smalls[7],
    )


def solution(mesh):
    rows, matrix, vector = P("dev", None), P(None, "dev", None), P(None, "dev")
    pairs = (matrix, vector) * 4
    return jax.shard_map(
        on_device,
        mesh=mesh,
        in_specs=(rows, P(), rows, *pairs, vector, vector, vector, vector),
        out_specs=(rows, rows, *pairs, vector, vector, vector, vector),
        check_vma=False,
    )
```
